32 devices in a mesh: gx: 4 (over z), gy: 2 (over y), gz: 4 (over x, core).
Axes of the slice: x: 2, y: 2, z: 4, core: 2. Of those that a mesh axis runs over, the one named last changes fastest.
Arguments:
- features: bfloat16 [16, 128, 64, 256], P(None, ('gx', 'gy', 'gz')), may hold values from -6 to 6
- score_filter_weight: bfloat16 [2, 16, 3, 3, 3], replicated, may hold values from -0.3125 to 0.3125
- tv_weight: float32 [128, 64, 256], P('gz', 'gx', 'gy'), may hold values from 0.05 to 0.5
Outputs:
- labels: float32 [128, 64, 256], P('gz', 'gx', 'gy')
- source_flow: float32 [128, 64, 256], P('gz', 'gx', 'gy')
The draws below stay inside these ranges and needn't reach their ends.
All inputs are finite; a program needn't handle non-finite values.
Results may differ from the reference program's by a relative error of at most 0.0003.
Values may be sent and summed in bfloat16 or wider, within the bound.
No kernel may reach another device: no remote copies, remote signals or barrier semaphores. Data moves between devices by JAX's collectives and lax.ppermute only.
A program may use at most 64 MiB of HBM per device.

```python
import math
import jax
import jax.numpy as jnp
from jax import lax

CHANNELS = 16
ITERS = 3
NX = 64
NY = 256
NZ = 128


def level_of(stream_key, shape, cuts, low, largest):
    loudness, own = 1.0, jax.random.fold_in(stream_key, 6)
    for position, parts in cuts:
        steps = jnp.exp(jax.random.uniform(jax.random.fold_in(own, position), (parts,), jnp.float32, low / len(cuts), largest / len(cuts)))
        loudness = loudness * jnp.repeat(steps, shape[position] // parts).reshape([-1 if axis == position else 1 for axis in range(len(shape))])
    return loudness


def normal_values(rng, dims, width, bound, shards=(), kind=jnp.bfloat16):
    gain = level_of(rng, dims, shards, -0.22, 0.18) if shards else 1.0
    entries = jax.random.normal(rng, dims, jnp.float32) * width * gain
    return jnp.minimum(jnp.maximum(entries, -bound), bound).astype(kind)


def setup_inputs(seed: int = 0) -> dict:
    key_list = jax.random.split(jax.random.key(seed), 4)
    return {
        "features": normal_values(key_list[0], (CHANNELS, NZ, NX, NY), 1.0, 6.0, ((1, 32),)),
        "score_filter_weight": normal_values(key_list[1], (2, CHANNELS, 3, 3, 3), (27 * CHANNELS) ** -0.5, 0.3125),
        "tv_weight": jnp.clip(jnp.exp(math.log(0.5) - 2.3025851 * jax.random.uniform(key_list[2], (NZ, NX, NY), jnp.float32) ** level_of(key_list[2], (NZ, NX, NY), ((0, 4), (1, 4), (2, 2)), -0.2, 0.2)), 0.05, 0.5),
    }


penalty = 0.3
step_size = 0.11

def capacity_fields(features, score_filter_weight):
    depth_len = features.shape[1]
    padded = jnp.pad(features, ((0, 0), (1, 1), (0, 0), (0, 0)))
    kernel = score_filter_weight.astype(jnp.float32)

    def plane(plane_id):
        window = lax.dynamic_slice_in_dim(padded, plane_id, 3, 1).astype(jnp.float32)
        result = lax.conv_general_dilated(window[None], kernel, (1, 1, 1), ((0, 0), (1, 1), (1, 1)), dimension_numbers=('NCDHW', 'OIDHW', 'NCDHW'), precision=lax.Precision.HIGHEST)
        return result[0, :, 0]
    planes = lax.map(plane, jnp.arange(depth_len, dtype=jnp.int32))
    return jax.nn.softplus(jnp.transpose(planes, (1, 0, 2, 3)))

def ahead(values, axis_id):
    length = values.shape[axis_id]
    remain = lax.slice_in_dim(values, 1, length, axis=axis_id)
    empty_border = jnp.zeros_like(lax.slice_in_dim(values, 0, 1, axis=axis_id))
    return jnp.concatenate([remain, empty_border], axis_id)

def behind(values, axis_id):
    length = values.shape[axis_id]
    remain = lax.slice_in_dim(values, 0, length - 1, axis=axis_id)
    empty_border = jnp.zeros_like(lax.slice_in_dim(values, 0, 1, axis=axis_id))
    return jnp.concatenate([empty_border, remain], axis_id)

def reference(features, score_filter_weight, tv_weight):
    edge_capacity = capacity_fields(features, score_filter_weight)
    source_cap = edge_capacity[0]
    sink_cap = edge_capacity[1]
    grid_shape = source_cap.shape
    inside = [lax.broadcasted_iota(jnp.int32, grid_shape, axis_id) < grid_shape[axis_id] - 1 for axis_id in range(3)]
    source_flow = jnp.minimum(source_cap, sink_cap)
    sink_flow = source_flow
    labels = jax.nn.sigmoid(source_cap - sink_cap)
    divergence = jnp.zeros(grid_shape, jnp.float32)
    edge_flows = [jnp.zeros(grid_shape, jnp.float32) for axis_id in range(3)]
    for iteration in range(ITERS):
        pressure = divergence - (source_flow - sink_flow + labels / penalty)
        updated = []
        for axis_id in range(3):
            moved = edge_flows[axis_id] + step_size * (ahead(pressure, axis_id) - pressure)
            updated.append(jnp.where(inside[axis_id], moved, jnp.float32(0.0)))
        flow_magnitude = jnp.sqrt(updated[0] * updated[0] + updated[1] * updated[1] + updated[2] * updated[2])
        factor = tv_weight / jnp.maximum(flow_magnitude, tv_weight)
        edge_flows = [flow_part * factor for flow_part in updated]
        divergence = edge_flows[0] - behind(edge_flows[0], 0) + (edge_flows[1] - behind(edge_flows[1], 1)) + (edge_flows[2] - behind(edge_flows[2], 2))
        source_flow = jnp.minimum(divergence - labels / penalty + sink_flow + 1.0 / penalty, source_cap)
        sink_flow = jnp.minimum(-divergence + source_flow + labels / penalty, sink_cap)
        labels = labels - penalty * (divergence + sink_flow - source_flow)
    return (labels, source_flow)
```

```python
import functools

import jax
import jax.numpy as jnp
from jax import lax
from jax.experimental import pallas as pl
from jax.experimental.pallas import tpu as pltpu
from jax.sharding import PartitionSpec as P

ITERS = 3
AXES = ("gx", "gy", "gz")

penalty = 0.3
step_size = 0.11


VMEM = pl.BlockSpec(memory_space=pltpu.VMEM)
SMEM = pl.BlockSpec(memory_space=pltpu.SMEM)
PARAMS = pltpu.CompilerParams(vmem_limit_bytes=56 * 1024 * 1024)


def with_halo(shard, sides, width):
    for axis, dim in sides:
        peers, length = (lax.axis_size(axis), shard.shape[dim])
        up = [(i, (i + 1) % peers) for i in range(peers - 1)]
        down = [(j, i) for i, j in up]
        last = lax.slice_in_dim(shard, length - width, length, axis=dim)
        leading = lax.slice_in_dim(shard, 0, width, axis=dim)
        before = lax.ppermute(last, axis, up)
        after = lax.ppermute(leading, axis, down)
        shard = jnp.concatenate([before, shard, after], axis=dim)
    return shard


def moved(values, offset, axis_id):
    if offset == 0:
        return values
    length = values.shape[axis_id]
    empty_border = jnp.zeros_like(lax.slice_in_dim(values, 0, 1, axis=axis_id))
    if offset > 0:
        return jnp.concatenate(
            [lax.slice_in_dim(values, 1, length, axis=axis_id), empty_border], axis_id
        )
    return jnp.concatenate(
        [empty_border, lax.slice_in_dim(values, 0, length - 1, axis=axis_id)], axis_id
    )


def plane_taps(slab, weights):
    kernel = jnp.transpose(weights, (2, 3, 0, 1)).reshape(18, weights.shape[1])
    products = jnp.einsum("kc,czxy->kzxy", kernel, slab, preferred_element_type=jnp.float32)
    products = products.reshape((3, 3, 2) + slab.shape[1:])
    summed = None
    for row_tap in range(3):
        for column_tap in range(3):
            term = moved(moved(products[row_tap, column_tap], row_tap - 1, 2), column_tap - 1, 3)
            summed = term if summed is None else summed + term
    return summed


def on_bricks(features, score_filter_weight, tv_weight):
    depth_len = features.shape[1]
    padded = with_halo(features, ((AXES, 1),), 1)
    response = None
    for depth_tap in range(3):
        window = lax.slice_in_dim(padded, depth_tap, depth_tap + depth_len, axis=1)
        term = plane_taps(window, score_filter_weight[:, :, depth_tap])
        response = term if response is None else response + term
    lifted = response.reshape((2, 1, 1) + response.shape[1:])
    by_plane = lax.all_to_all(
        lax.all_to_all(lifted, "gx", split_axis=4, concat_axis=1, tiled=True),
        "gy",
        split_axis=5,
        concat_axis=2,
        tiled=True,
    )
    edge_capacity = jax.nn.softplus(by_plane)
    sorted_by_depth = lax.all_to_all(edge_capacity, "gz", split_axis=1, concat_axis=3, tiled=True)
    brick = sorted_by_depth.reshape(
        (
            2,
            sorted_by_depth.shape[2] * sorted_by_depth.shape[3],
            sorted_by_depth.shape[4],
            sorted_by_depth.shape[5],
        )
    )
    source_cap = brick[0]
    sink_cap = brick[1]
    grid_shape = source_cap.shape
    starts = (
        lax.axis_index("gz") * grid_shape[0],
        lax.axis_index("gx") * grid_shape[1],
        lax.axis_index("gy") * grid_shape[2],
    )
    totals = (
        grid_shape[0] * lax.axis_size("gz"),
        grid_shape[1] * lax.axis_size("gx"),
        grid_shape[2] * lax.axis_size("gy"),
    )
    region = tuple((length + 1 for length in grid_shape))
    inside = []
    for axis_id in range(3):
        position = starts[axis_id] - 1 + lax.broadcasted_iota(jnp.int32, region, axis_id)
        inside.append((position >= 0) & (position <= totals[axis_id] - 2))
    source_flow = jnp.minimum(source_cap, sink_cap)
    sink_flow = source_flow
    labels = jax.nn.sigmoid(source_cap - sink_cap)
    divergence = jnp.zeros(grid_shape, jnp.float32)
    edge_flows = [jnp.zeros(grid_shape, jnp.float32) for axis_id in range(3)]
    for iteration in range(ITERS):
        pressure = divergence - (source_flow - sink_flow + labels / penalty)
        state = jnp.stack([pressure, edge_flows[0], edge_flows[1], edge_flows[2], tv_weight], 0)
        widened_block = with_halo(state, (("gx", 2), ("gy", 3), ("gz", 1)), 1)
        base = widened_block[:, :-1, :-1, :-1]
        updated = []
        for axis_id in range(3):
            picks = [slice(0, -1), slice(0, -1), slice(0, -1)]
            picks[axis_id] = slice(1, None)
            next_pressure = widened_block[0][tuple(picks)]
            shifted = base[1 + axis_id] + step_size * (next_pressure - base[0])
            updated.append(jnp.where(inside[axis_id], shifted, jnp.float32(0.0)))
        flow_magnitude = jnp.sqrt(
            updated[0] * updated[0] + updated[1] * updated[1] + updated[2] * updated[2]
        )
        factor = base[4] / jnp.maximum(flow_magnitude, base[4])
        projected = [
            jnp.where(inside[axis_id], updated[axis_id] * factor, jnp.float32(0.0))
            for axis_id in range(3)
        ]
        edge_flows = [flow_part[1:, 1:, 1:] for flow_part in projected]
        divergence = (
            edge_flows[0]
            - projected[0][:-1, 1:, 1:]
            + (edge_flows[1] - projected[1][1:, :-1, 1:])
            + (edge_flows[2] - projected[2][1:, 1:, :-1])
        )
        source_flow = jnp.minimum(
            divergence - labels / penalty + sink_flow + 1.0 / penalty, source_cap
        )
        sink_flow = jnp.minimum(-divergence + source_flow + labels / penalty, sink_cap)
        labels = labels - penalty * (divergence + sink_flow - source_flow)
    return (labels, source_flow)


def conv_kernel(scalars, w_ref, f_ref, own_ref, near_ref, far_ref, band):
    channels, depth, rows, columns = f_ref.shape
    parity = scalars[0]
    width = channels * rows
    channel = lax.broadcasted_iota(jnp.int32, (channels, width), 0)
    position = lax.broadcasted_iota(jnp.int32, (channels, width), 1)
    spread = (position >= channel * rows) & (position < (channel + 1) * rows)
    spread = jnp.where(spread, 1.0, 0.0).astype(jnp.bfloat16)
    weights = jnp.dot(w_ref[...], spread, preferred_element_type=jnp.float32)
    column = lax.broadcasted_iota(jnp.int32, (rows, width), 1)
    offset = lax.rem(column, rows) - lax.broadcasted_iota(jnp.int32, (rows, width), 0)
    for dz in range(3):
        for j in range(3):
            for o in range(2):
                value = jnp.zeros((rows, width), jnp.float32)
                for i in range(3):
                    r = ((dz * 3 + i) * 3 + j) * 2 + o
                    value = jnp.where(offset == i - 1, weights[r : r + 1, :], value)
                start = (j * 2 + o) * rows
                band[dz, start : start + rows, :] = value.astype(jnp.bfloat16)
    lane = lax.broadcasted_iota(jnp.int32, (2 * rows, columns), 1)
    for z in range(-1, depth + 1):
        taps = None
        for dz in range(3):
            plane = z + dz - 1
            if 0 <= plane < depth:
                term = jnp.dot(
                    band[dz],
                    f_ref[:, plane].reshape(width, columns),
                    preferred_element_type=jnp.float32,
                )
                taps = term if taps is None else taps + term
        before = pltpu.roll(taps[: 2 * rows], 1, 1)
        after = pltpu.roll(taps[4 * rows :], columns - 1, 1)
        total = (
            taps[2 * rows : 4 * rows]
            + jnp.where(lane >= 1, before, 0.0)
            + jnp.where(lane < columns - 1, after, 0.0)
        )
        own_ref[z + 1] = total.reshape(2, rows, columns)
    near_ref[...] = own_ref[pl.ds(2 - 2 * parity, depth)]
    far_ref[...] = own_ref[pl.ds(2 * parity, depth)]


def softplus(v):
    e = jnp.exp(-jnp.abs(v))
    series = e * (1.0 - e * (0.5 - e * (1.0 / 3.0 - e * 0.25)))
    return jnp.maximum(v, 0.0) + jnp.where(e < 0.02, series, jnp.log(1.0 + e))


def flow_kernel(
    total_depth,
    scalars,
    own_ref,
    near_ref,
    far_ref,
    tv_own_ref,
    tv_got_ref,
    keep_ref,
    give_ref,
    resp,
    tv,
    cap_s,
    cap_t,
    flow_s,
    flow_t,
    lab,
    press,
    q0,
    q1,
    q2,
    out,
):
    planes, _, rows, columns = own_ref.shape
    depth = planes - 2
    half = rows // 2
    parity = scalars[0]
    first = scalars[1]
    resp[3 - 1 : 3 + depth + 1] = own_ref[...]
    resp[0:2] = jnp.zeros((2, 2, rows, columns), jnp.float32)
    resp[depth + 4 : depth + 6] = jnp.zeros((2, 2, rows, columns), jnp.float32)
    near_at = depth + 2 - (depth + 2) * parity
    far_at = (depth + 2) * parity
    resp[pl.ds(near_at, 4)] = resp[pl.ds(near_at, 4)] + near_ref[...]
    resp[pl.ds(far_at, 4)] = resp[pl.ds(far_at, 4)] + far_ref[...]
    tv[:, pl.ds(pl.multiple_of(parity * half, half), half), :] = tv_own_ref[...]
    tv[:, pl.ds(pl.multiple_of(half - parity * half, half), half), :] = tv_got_ref[...]

    def start(i, carry):
        source_cap = softplus(resp[i, 0])
        sink_cap = softplus(resp[i, 1])
        flow = jnp.minimum(source_cap, sink_cap)
        labels = jax.nn.sigmoid(source_cap - sink_cap)
        cap_s[i] = source_cap
        cap_t[i] = sink_cap
        flow_s[i] = flow
        flow_t[i] = flow
        lab[i] = labels
        press[i] = -(labels / penalty)
        return carry

    lax.fori_loop(0, depth + 6, start, 0)
    row = lax.broadcasted_iota(jnp.int32, (rows, columns), 0)
    column = lax.broadcasted_iota(jnp.int32, (rows, columns), 1)
    row_in = row < rows - 1
    column_in = column < columns - 1

    def edges(i, fresh):
        z = first + i - 3
        p = press[i]
        deep = step_size * (press[i + 1] - p)
        down = step_size * (pltpu.roll(p, rows - 1, 0) - p)
        right = step_size * (pltpu.roll(p, columns - 1, 1) - p)
        if not fresh:
            deep, down, right = q0[i] + deep, q1[i] + down, q2[i] + right
        inside = (z >= 0) & (z < total_depth - 1)
        deep = jnp.where(inside, deep, 0.0)
        down = jnp.where(row_in, down, 0.0)
        right = jnp.where(column_in, right, 0.0)
        weight = tv[i]
        magnitude = jnp.sqrt(deep * deep + down * down + right * right)
        factor = weight / jnp.maximum(magnitude, weight)
        deep, down, right = deep * factor, down * factor, right * factor
        deep = jnp.where(inside, deep, 0.0)
        q0[i] = deep
        q1[i] = down
        q2[i] = right
        return deep, down, right

    def cell(i, fresh, last):
        deep, down, right = edges(i, fresh)
        divergence = (
            deep - q0[i - 1] + (down - pltpu.roll(down, 1, 0)) + (right - pltpu.roll(right, 1, 1))
        )
        labels = lab[i]
        scaled = labels / penalty
        source_flow = jnp.minimum(divergence - scaled + flow_t[i] + 1.0 / penalty, cap_s[i])
        sink_flow = jnp.minimum(-divergence + source_flow + scaled, cap_t[i])
        labels = labels - penalty * (divergence + sink_flow - source_flow)
        if last:
            out[0, i - 3] = labels
            out[1, i - 3] = source_flow
        else:
            flow_t[i] = sink_flow
            lab[i] = labels
            press[i] = divergence - (source_flow - sink_flow + labels / penalty)

    for iteration in range(ITERS):
        fresh, last = iteration == 0, iteration == ITERS - 1
        edges(iteration, fresh)

        def step(i, carry):
            cell(i, fresh, last)
            return carry

        lax.fori_loop(iteration + 1, depth + 5 - iteration, step, 0)
    keep_ref[...] = out[:, :, pl.ds(pl.multiple_of(parity * half, half), half), :]
    give_ref[...] = out[:, :, pl.ds(pl.multiple_of(half - parity * half, half), half), :]


def pack_kernel(gy, scalars, keep_ref, got_ref, *message_refs):
    depth = keep_ref.shape[1]
    _, _, block_rows, block_columns = message_refs[0].shape
    parity, chip = scalars[0], scalars[2]
    for k, message in enumerate(message_refs):
        target = chip ^ k
        rows = pl.ds(pl.multiple_of(target // gy * block_rows, block_rows), block_rows)
        columns = pl.ds(pl.multiple_of(target % gy * block_columns, block_columns), block_columns)
        message[:, pl.ds(parity * depth, depth)] = keep_ref[:, :, rows, columns]
        message[:, pl.ds(depth - parity * depth, depth)] = got_ref[:, :, rows, columns]


def unpack_kernel(count, scalars, *refs):
    messages, (labels_ref, flow_ref) = refs[:count], refs[count:]
    planes = messages[0].shape[1]
    for k, message in enumerate(messages):
        at = pl.ds((scalars[3] ^ k) * planes, planes)
        labels_ref[at] = message[0]
        flow_ref[at] = message[1]


def tv_pack_kernel(scalars, tv_ref, near_ref, far_ref, *refs):
    messages, wide = refs[:-1], refs[-1]
    length = tv_ref.shape[0]
    parity = scalars[4]
    wide[3 : 3 + length] = tv_ref[...]

    @pl.when(parity == 0)
    def _():
        wide[length + 3 : length + 6] = near_ref[...]
        wide[0:3] = far_ref[...]

    @pl.when(parity == 1)
    def _():
        wide[length + 3 : length + 6] = far_ref[...]
        wide[0:3] = near_ref[...]

    planes = messages[0].shape[0]
    for k, message in enumerate(messages):
        message[...] = wide[pl.ds((scalars[3] ^ k) * (planes - 5), planes)]


def tv_unpack_kernel(gy, count, scalars, *refs):
    messages, (own_ref, give_ref, full) = refs[:count], refs[count:]
    planes, block_rows, block_columns = messages[0].shape
    depth = (planes - 5) // 2
    parity, chip = scalars[0], scalars[2]
    for k, message in enumerate(messages):
        target = chip ^ k
        rows = pl.ds(pl.multiple_of(target // gy * block_rows, block_rows), block_rows)
        columns = pl.ds(pl.multiple_of(target % gy * block_columns, block_columns), block_columns)
        full[:, rows, columns] = message[...]
    own_ref[...] = full[pl.ds(parity * depth, depth + 5)]
    give_ref[...] = full[pl.ds(depth - parity * depth, depth + 5)]


def call(kernel, out_shape, scratch, scalars, *operands):
    return pl.pallas_call(
        kernel,
        out_shape=[jax.ShapeDtypeStruct(shape, jnp.float32) for shape in out_shape],
        in_specs=[SMEM] + [VMEM] * len(operands),
        out_specs=[VMEM] * len(out_shape),
        scratch_shapes=scratch,
        compiler_params=PARAMS,
    )(scalars, *operands)


def scratch(*shape, dtype=jnp.float32):
    return pltpu.VMEM(shape, dtype)


def on_slabs(features, score_filter_weight, tv_weight):
    channels, depth, rows, columns = features.shape
    brick_depth, block_rows, block_columns = tv_weight.shape
    gx, gy, gz = (lax.axis_size(axis) for axis in AXES)
    slabs, chips = gx * gy * gz, gy * gz // 2
    half = rows // 2
    a, b, c = (lax.axis_index(axis) for axis in AXES)
    slab = (a * gy + b) * gz + c
    scalars = jnp.stack(
        [c % 2, slab * depth, b * (gz // 2) + c // 2, a % (gx // 2) * gy + b, c % 2]
    ).astype(jnp.int32)

    near = [(s, s ^ 1) for s in range(slabs)]
    far = [(s, s + 1) for s in range(1, slabs - 1, 2)]
    far = far + [(t, s) for s, t in far]
    gz_near = [(s, s ^ 1) for s in range(gz)]
    gz_far = [(s, s + 1) for s in range(1, gz - 1, 2)]
    gz_far = gz_far + [(t, s) for s, t in gz_far]

    def place(i, j, k):
        return (i * gy + j) * gz + k

    def to_bricks(k):
        pairs = []
        for i in range(gx):
            for j in range(gy):
                for m in range(gz):
                    target = (j * (gz // 2) + m // 2) ^ k
                    row_block = m % 2 * (gx // 2) + target // gy
                    pairs.append((place(i, j, m), place(row_block, target % gy, i)))
        return pairs

    routes = [to_bricks(k) for k in range(chips)]

    tv_last, tv_first = tv_weight[brick_depth - 3 :], tv_weight[:3]
    even = c % 2 == 0
    tv_near = lax.ppermute(jnp.where(even, tv_last, tv_first), "gz", gz_near)
    tv_far = lax.ppermute(jnp.where(even, tv_first, tv_last), "gz", gz_far)
    tv_messages = call(
        tv_pack_kernel,
        [(2 * depth + 5, block_rows, block_columns)] * chips,
        [scratch(brick_depth + 6, block_rows, block_columns)],
        scalars,
        tv_weight,
        tv_near,
        tv_far,
    )

    flat_weight = jnp.transpose(score_filter_weight, (2, 3, 4, 0, 1)).reshape(54, channels)
    message = (4, 2, rows, columns)
    own, near_out, far_out = call(
        conv_kernel,
        [(depth + 2, 2, rows, columns), message, message],
        [scratch(3, 6 * rows, channels * rows, dtype=jnp.bfloat16)],
        scalars,
        flat_weight,
        features,
    )
    far_in = lax.ppermute(far_out, AXES, far)
    near_in = lax.ppermute(near_out, AXES, near)

    tv_in = [
        lax.ppermute(piece, AXES, [(t, s) for s, t in routes[k]])
        for k, piece in enumerate(tv_messages)
    ]
    tv_half = (depth + 5, half, columns)
    tv_own, tv_give = call(
        functools.partial(tv_unpack_kernel, gy, chips),
        [tv_half, tv_half],
        [scratch(2 * depth + 5, half, columns)],
        scalars,
        *tv_in,
    )
    tv_got = lax.ppermute(tv_give, AXES, near)

    wide = (depth + 6, rows, columns)
    out_half = (2, depth, half, columns)
    keep, give = call(
        functools.partial(flow_kernel, slabs * depth),
        [out_half, out_half],
        [scratch(depth + 6, 2, rows, columns), scratch(depth + 5, rows, columns)]
        + [scratch(*wide)] * 9
        + [scratch(2, depth, rows, columns)],
        scalars,
        own,
        near_in,
        far_in,
        tv_own,
        tv_got,
    )
    got = lax.ppermute(give, AXES, near)
    messages = call(
        functools.partial(pack_kernel, gy),
        [(2, 2 * depth, block_rows, block_columns)] * chips,
        [],
        scalars,
        keep,
        got,
    )
    arrived = [lax.ppermute(piece, AXES, routes[k]) for k, piece in enumerate(messages)]
    labels, source_flow = call(
        functools.partial(unpack_kernel, chips),
        [tv_weight.shape, tv_weight.shape],
        [],
        scalars,
        *arrived,
    )
    return (labels, source_flow)


def shards(features, score_filter_weight, tv_weight):
    gx, gy, gz = (lax.axis_size(axis) for axis in AXES)
    chips = gy * gz // 2
    fits = (
        features.shape[1] == 4
        and gx == gz
        and gx % 2 == 0
        and chips & (chips - 1) == 0
        and tv_weight.shape[1] % 8 == 0
        and tv_weight.shape[2] % 128 == 0
    )
    return (on_slabs if fits else on_bricks)(features, score_filter_weight, tv_weight)


def solution(mesh):
    return jax.shard_map(
        shards,
        mesh=mesh,
        in_specs=(P(None, ("gx", "gy", "gz"), None, None), P(), P("gz", "gx", "gy")),
        out_specs=(P("gz", "gx", "gy"), P("gz", "gx", "gy")),
        check_vma=False,
    )
```

```python
import functools

import jax
import jax.numpy as jnp
from jax import lax
from jax.experimental import pallas as pl
from jax.experimental.pallas import tpu as pltpu
from jax.sharding import PartitionSpec as P

ITERS = 3
AXES = ("gx", "gy", "gz")

penalty = 0.3
step_size = 0.11
inverse_penalty = 1.0 / penalty


VMEM = pl.BlockSpec(memory_space=pltpu.VMEM)
SMEM = pl.BlockSpec(memory_space=pltpu.SMEM)


def with_halo(shard, sides, width):
    for axis, dim in sides:
        peers, length = (lax.axis_size(axis), shard.shape[dim])
        up = [(i, (i + 1) % peers) for i in range(peers - 1)]
        down = [(j, i) for i, j in up]
        last = lax.slice_in_dim(shard, length - width, length, axis=dim)
        leading = lax.slice_in_dim(shard, 0, width, axis=dim)
        before = lax.ppermute(last, axis, up)
        after = lax.ppermute(leading, axis, down)
        shard = jnp.concatenate([before, shard, after], axis=dim)
    return shard


def moved(values, offset, axis_id):
    if offset == 0:
        return values
    length = values.shape[axis_id]
    empty_border = jnp.zeros_like(lax.slice_in_dim(values, 0, 1, axis=axis_id))
    if offset > 0:
        return jnp.concatenate(
            [lax.slice_in_dim(values, 1, length, axis=axis_id), empty_border], axis_id
        )
    return jnp.concatenate(
        [empty_border, lax.slice_in_dim(values, 0, length - 1, axis=axis_id)], axis_id
    )


def plane_taps(slab, weights):
    kernel = jnp.transpose(weights, (2, 3, 0, 1)).reshape(18, weights.shape[1])
    products = jnp.einsum("kc,czxy->kzxy", kernel, slab, preferred_element_type=jnp.float32)
    products = products.reshape((3, 3, 2) + slab.shape[1:])
    summed = None
    for row_tap in range(3):
        for column_tap in range(3):
            term = moved(moved(products[row_tap, column_tap], row_tap - 1, 2), column_tap - 1, 3)
            summed = term if summed is None else summed + term
    return summed


def on_bricks(features, score_filter_weight, tv_weight):
    depth_len = features.shape[1]
    padded = with_halo(features, ((AXES, 1),), 1)
    response = None
    for depth_tap in range(3):
        window = lax.slice_in_dim(padded, depth_tap, depth_tap + depth_len, axis=1)
        term = plane_taps(window, score_filter_weight[:, :, depth_tap])
        response = term if response is None else response + term
    lifted = response.reshape((2, 1, 1) + response.shape[1:])
    by_plane = lax.all_to_all(
        lax.all_to_all(lifted, "gx", split_axis=4, concat_axis=1, tiled=True),
        "gy",
        split_axis=5,
        concat_axis=2,
        tiled=True,
    )
    edge_capacity = jax.nn.softplus(by_plane)
    sorted_by_depth = lax.all_to_all(edge_capacity, "gz", split_axis=1, concat_axis=3, tiled=True)
    brick = sorted_by_depth.reshape(
        (
            2,
            sorted_by_depth.shape[2] * sorted_by_depth.shape[3],
            sorted_by_depth.shape[4],
            sorted_by_depth.shape[5],
        )
    )
    source_cap = brick[0]
    sink_cap = brick[1]
    grid_shape = source_cap.shape
    starts = (
        lax.axis_index("gz") * grid_shape[0],
        lax.axis_index("gx") * grid_shape[1],
        lax.axis_index("gy") * grid_shape[2],
    )
    totals = (
        grid_shape[0] * lax.axis_size("gz"),
        grid_shape[1] * lax.axis_size("gx"),
        grid_shape[2] * lax.axis_size("gy"),
    )
    region = tuple((length + 1 for length in grid_shape))
    inside = []
    for axis_id in range(3):
        position = starts[axis_id] - 1 + lax.broadcasted_iota(jnp.int32, region, axis_id)
        inside.append((position >= 0) & (position <= totals[axis_id] - 2))
    source_flow = jnp.minimum(source_cap, sink_cap)
    sink_flow = source_flow
    labels = jax.nn.sigmoid(source_cap - sink_cap)
    divergence = jnp.zeros(grid_shape, jnp.float32)
    edge_flows = [jnp.zeros(grid_shape, jnp.float32) for axis_id in range(3)]
    for iteration in range(ITERS):
        pressure = divergence - (source_flow - sink_flow + labels / penalty)
        state = jnp.stack([pressure, edge_flows[0], edge_flows[1], edge_flows[2], tv_weight], 0)
        widened_block = with_halo(state, (("gx", 2), ("gy", 3), ("gz", 1)), 1)
        base = widened_block[:, :-1, :-1, :-1]
        updated = []
        for axis_id in range(3):
            picks = [slice(0, -1), slice(0, -1), slice(0, -1)]
            picks[axis_id] = slice(1, None)
            next_pressure = widened_block[0][tuple(picks)]
            shifted = base[1 + axis_id] + step_size * (next_pressure - base[0])
            updated.append(jnp.where(inside[axis_id], shifted, jnp.float32(0.0)))
        flow_magnitude = jnp.sqrt(
            updated[0] * updated[0] + updated[1] * updated[1] + updated[2] * updated[2]
        )
        factor = base[4] / jnp.maximum(flow_magnitude, base[4])
        projected = [
            jnp.where(inside[axis_id], updated[axis_id] * factor, jnp.float32(0.0))
            for axis_id in range(3)
        ]
        edge_flows = [flow_part[1:, 1:, 1:] for flow_part in projected]
        divergence = (
            edge_flows[0]
            - projected[0][:-1, 1:, 1:]
            + (edge_flows[1] - projected[1][1:, :-1, 1:])
            + (edge_flows[2] - projected[2][1:, 1:, :-1])
        )
        source_flow = jnp.minimum(
            divergence - labels / penalty + sink_flow + 1.0 / penalty, source_cap
        )
        sink_flow = jnp.minimum(-divergence + source_flow + labels / penalty, sink_cap)
        labels = labels - penalty * (divergence + sink_flow - source_flow)
    return (labels, source_flow)


def conv_kernel(place_of, index,  w_ref, f_ref, own_ref, near_ref, far_ref, band):
    channels, depth, rows, columns = f_ref.shape
    parity = place_of(index)[0]
    width = channels * rows
    channel = lax.broadcasted_iota(jnp.int32, (channels, width), 0)
    position = lax.broadcasted_iota(jnp.int32, (channels, width), 1)
    spread = (position >= channel * rows) & (position < (channel + 1) * rows)
    spread = jnp.where(spread, 1.0, 0.0).astype(jnp.bfloat16)
    taps_of = w_ref[...].astype(jnp.float32).reshape(27 * 2, channels).astype(jnp.bfloat16)
    weights = jnp.dot(taps_of, spread, preferred_element_type=jnp.float32)
    column = lax.broadcasted_iota(jnp.int32, (rows, width), 1)
    offset = lax.rem(column, rows) - lax.broadcasted_iota(jnp.int32, (rows, width), 0)
    for dz in range(3):
        for j in range(3):
            for o in range(2):
                value = jnp.zeros((rows, width), jnp.float32)
                for i in range(3):
                    r = ((dz * 3 + i) * 3 + j) * 2 + o
                    value = jnp.where(offset == i - 1, weights[r : r + 1, :], value)
                start = (j * 2 + o) * rows
                band[dz, start : start + rows, :] = value.astype(jnp.bfloat16)
    lane = lax.broadcasted_iota(jnp.int32, (2 * rows, columns), 1)
    for z in range(-1, depth + 1):
        taps = None
        for dz in range(3):
            plane = z + dz - 1
            if 0 <= plane < depth:
                term = jnp.dot(
                    band[dz],
                    f_ref[:, plane].reshape(width, columns),
                    preferred_element_type=jnp.float32,
                )
                taps = term if taps is None else taps + term
        before = pltpu.roll(taps[: 2 * rows], 1, 1)
        after = pltpu.roll(taps[4 * rows :], columns - 1, 1)
        total = (
            taps[2 * rows : 4 * rows]
            + jnp.where(lane >= 1, before, 0.0)
            + jnp.where(lane < columns - 1, after, 0.0)
        )
        own_ref[z + 1] = total.reshape(2, rows, columns)
    near_ref[...] = own_ref[pl.ds(2 - 2 * parity, depth)]
    far_ref[...] = own_ref[pl.ds(2 * parity, depth)]


def softplus(v):
    e = jnp.exp(-jnp.abs(v))
    series = e * (1.0 - e * (0.5 - e * (1.0 / 3.0 - e * 0.25)))
    return jnp.maximum(v, 0.0) + jnp.where(e < 0.02, series, jnp.log(1.0 + e))


def flow_kernel(
    total_depth,
    place_of,
    index,
    own_ref,
    near_ref,
    far_ref,
    tv_own_ref,
    tv_got_ref,
    keep_ref,
    give_ref,
    resp,
    tv,
    cap_s,
    cap_t,
    flow_s,
    flow_t,
    lab,
    press,
    q0,
    q1,
    q2,
    out,
):
    planes, _, rows, columns = own_ref.shape
    depth = planes - 2
    half = rows // 2
    parity, first = place_of(index)[:2]
    resp[3 - 1 : 3 + depth + 1] = own_ref[...]
    resp[0:2] = jnp.zeros((2, 2, rows, columns), jnp.float32)
    resp[depth + 4 : depth + 6] = jnp.zeros((2, 2, rows, columns), jnp.float32)
    near_at = depth + 2 - (depth + 2) * parity
    far_at = (depth + 2) * parity
    resp[pl.ds(near_at, 4)] = resp[pl.ds(near_at, 4)] + near_ref[...]
    resp[pl.ds(far_at, 4)] = resp[pl.ds(far_at, 4)] + far_ref[...]
    tv[:, pl.ds(pl.multiple_of(parity * half, half), half), :] = tv_own_ref[...]
    tv[:, pl.ds(pl.multiple_of(half - parity * half, half), half), :] = tv_got_ref[...]

    def start(i, carry):
        source_cap = softplus(resp[i, 0])
        sink_cap = softplus(resp[i, 1])
        flow = jnp.minimum(source_cap, sink_cap)
        labels = jax.nn.sigmoid(source_cap - sink_cap)
        cap_s[i] = source_cap
        cap_t[i] = sink_cap
        flow_s[i] = flow
        flow_t[i] = flow
        lab[i] = labels
        press[i] = -(labels * inverse_penalty)
        return carry

    lax.fori_loop(0, depth + 6, start, 0)
    row = lax.broadcasted_iota(jnp.int32, (rows, columns), 0)
    column = lax.broadcasted_iota(jnp.int32, (rows, columns), 1)
    row_in = row < rows - 1
    column_in = column < columns - 1

    def edges(i, fresh):
        z = first + i - 3
        p = press[i]
        deep = step_size * (press[i + 1] - p)
        down = step_size * (pltpu.roll(p, rows - 1, 0) - p)
        right = step_size * (pltpu.roll(p, columns - 1, 1) - p)
        if not fresh:
            deep, down, right = q0[i] + deep, q1[i] + down, q2[i] + right
        inside = (z >= 0) & (z < total_depth - 1)
        deep = jnp.where(inside, deep, 0.0)
        down = jnp.where(row_in, down, 0.0)
        right = jnp.where(column_in, right, 0.0)
        weight = tv[i]
        squares = deep * deep + down * down + right * right
        factor = jnp.minimum(weight * lax.rsqrt(squares), 1.0)
        deep, down, right = deep * factor, down * factor, right * factor
        deep = jnp.where(inside, deep, 0.0)
        q0[i] = deep
        q1[i] = down
        q2[i] = right
        return deep, down, right

    def cell(i, fresh, last):
        deep, down, right = edges(i, fresh)
        divergence = (
            deep - q0[i - 1] + (down - pltpu.roll(down, 1, 0)) + (right - pltpu.roll(right, 1, 1))
        )
        labels = lab[i]
        scaled = labels * inverse_penalty
        source_flow = jnp.minimum(divergence - scaled + flow_t[i] + inverse_penalty, cap_s[i])
        sink_flow = jnp.minimum(-divergence + source_flow + scaled, cap_t[i])
        labels = labels - penalty * (divergence + sink_flow - source_flow)
        if last:
            out[0, i - 3] = labels
            out[1, i - 3] = source_flow
        else:
            flow_t[i] = sink_flow
            lab[i] = labels
            press[i] = divergence - (source_flow - sink_flow + labels * inverse_penalty)

    for iteration in range(ITERS):
        fresh, last = iteration == 0, iteration == ITERS - 1
        edges(iteration, fresh)

        def step(i, carry):
            cell(i, fresh, last)
            return carry

        lax.fori_loop(iteration + 1, depth + 5 - iteration, step, 0)
    keep_ref[...] = out[:, :, pl.ds(pl.multiple_of(parity * half, half), half), :]
    give_ref[...] = out[:, :, pl.ds(pl.multiple_of(half - parity * half, half), half), :]


def pack_kernel(gy, place_of, index, keep_ref, got_ref, *message_refs):
    depth = keep_ref.shape[1]
    _, _, block_rows, block_columns = message_refs[0].shape
    parity, _, chip, _ = place_of(index)
    for k, message in enumerate(message_refs):
        target = chip ^ k
        rows = pl.ds(pl.multiple_of(target // gy * block_rows, block_rows), block_rows)
        columns = pl.ds(pl.multiple_of(target % gy * block_columns, block_columns), block_columns)
        message[:, pl.ds(parity * depth, depth)] = keep_ref[:, :, rows, columns]
        message[:, pl.ds(depth - parity * depth, depth)] = got_ref[:, :, rows, columns]


def unpack_kernel(count, place_of, index, *refs):
    messages, (labels_ref, flow_ref) = refs[:count], refs[count:]
    planes = messages[0].shape[1]
    brick = place_of(index)[3]
    for k, message in enumerate(messages):
        at = pl.ds((brick ^ k) * planes, planes)
        labels_ref[at] = message[0]
        flow_ref[at] = message[1]


def tv_pack_kernel(place_of, index, tv_ref, near_ref, far_ref, *refs):
    messages, wide = refs[:-1], refs[-1]
    length = tv_ref.shape[0]
    parity, _, _, brick = place_of(index)
    wide[3 : 3 + length] = tv_ref[...]

    @pl.when(parity == 0)
    def _():
        wide[length + 3 : length + 6] = near_ref[...]
        wide[0:3] = far_ref[...]

    @pl.when(parity == 1)
    def _():
        wide[length + 3 : length + 6] = far_ref[...]
        wide[0:3] = near_ref[...]

    planes = messages[0].shape[0]
    for k, message in enumerate(messages):
        message[...] = wide[pl.ds((brick ^ k) * (planes - 5), planes)]


def tv_unpack_kernel(gy, count, place_of, index, *refs):
    messages, (own_ref, give_ref, full) = refs[:count], refs[count:]
    planes, block_rows, block_columns = messages[0].shape
    depth = (planes - 5) // 2
    parity, _, chip, _ = place_of(index)
    for k, message in enumerate(messages):
        target = chip ^ k
        rows = pl.ds(pl.multiple_of(target // gy * block_rows, block_rows), block_rows)
        columns = pl.ds(pl.multiple_of(target % gy * block_columns, block_columns), block_columns)
        full[:, rows, columns] = message[...]
    own_ref[...] = full[pl.ds(parity * depth, depth + 5)]
    give_ref[...] = full[pl.ds(depth - parity * depth, depth + 5)]


def places(sizes, depth, index_ref):
    gx, gy, gz = sizes
    slab = index_ref[0]
    c = lax.rem(slab, gz)
    b = lax.rem(lax.div(slab, gz), gy)
    a = lax.div(slab, gy * gz)
    parity = lax.rem(c, 2)
    return (
        parity,
        slab * depth,
        b * (gz // 2) + lax.div(c, 2),
        lax.rem(a, gx // 2) * gy + b,
    )


def call(kernel, out_shape, scratch, scalars, *operands, mib=8):
    return pl.pallas_call(
        kernel,
        out_shape=[jax.ShapeDtypeStruct(shape, jnp.float32) for shape in out_shape],
        in_specs=[SMEM] + [VMEM] * len(operands),
        out_specs=[VMEM] * len(out_shape),
        scratch_shapes=scratch,
        compiler_params=pltpu.CompilerParams(vmem_limit_bytes=mib * 1024 * 1024),
    )(scalars, *operands)


def scratch(*shape, dtype=jnp.float32):
    return pltpu.VMEM(shape, dtype)


def on_slabs(features, score_filter_weight, tv_weight):
    channels, depth, rows, columns = features.shape
    brick_depth, block_rows, block_columns = tv_weight.shape
    gx, gy, gz = (lax.axis_size(axis) for axis in AXES)
    slabs, chips = gx * gy * gz, gy * gz // 2
    half = rows // 2
    a, b, c = (lax.axis_index(axis) for axis in AXES)
    slab = (a * gy + b) * gz + c
    place_of = functools.partial(places, (gx, gy, gz), depth)
    scalars = lax.axis_index(AXES).astype(jnp.int32).reshape(1)

    near = [(s, s ^ 1) for s in range(slabs)]
    far = [(s, s + 1) for s in range(1, slabs - 1, 2)]
    far = far + [(t, s) for s, t in far]
    gz_near = [(s, s ^ 1) for s in range(gz)]
    gz_far = [(s, s + 1) for s in range(1, gz - 1, 2)]
    gz_far = gz_far + [(t, s) for s, t in gz_far]

    def place(i, j, k):
        return (i * gy + j) * gz + k

    def to_bricks(k):
        pairs = []
        for i in range(gx):
            for j in range(gy):
                for m in range(gz):
                    target = (j * (gz // 2) + m // 2) ^ k
                    row_block = m % 2 * (gx // 2) + target // gy
                    pairs.append((place(i, j, m), place(row_block, target % gy, i)))
        return pairs

    routes = [to_bricks(k) for k in range(chips)]

    tv_last, tv_first = tv_weight[brick_depth - 3 :], tv_weight[:3]
    even = c % 2 == 0
    tv_near = lax.ppermute(jnp.where(even, tv_last, tv_first), "gz", gz_near)
    tv_far = lax.ppermute(jnp.where(even, tv_first, tv_last), "gz", gz_far)
    tv_messages = call(
        functools.partial(tv_pack_kernel, place_of),
        [(2 * depth + 5, block_rows, block_columns)] * chips,
        [scratch(brick_depth + 6, block_rows, block_columns)],
        scalars,
        tv_weight,
        tv_near,
        tv_far,
    )

    flat_weight = jnp.transpose(score_filter_weight, (2, 3, 4, 0, 1))
    message = (4, 2, rows, columns)
    own, near_out, far_out = call(
        functools.partial(conv_kernel, place_of),
        [(depth + 2, 2, rows, columns), message, message],
        [scratch(3, 6 * rows, channels * rows, dtype=jnp.bfloat16)],
        scalars,
        flat_weight,
        features,
        mib=14,
    )
    tv_messages, far_out, near_out = lax.optimization_barrier((tv_messages, far_out, near_out))
    far_in = lax.ppermute(far_out, AXES, far)
    near_in = lax.ppermute(near_out, AXES, near)

    tv_in = [
        lax.ppermute(piece, AXES, [(t, s) for s, t in routes[k]])
        for k, piece in enumerate(tv_messages)
    ]
    tv_half = (depth + 5, half, columns)
    tv_own, tv_give = call(
        functools.partial(tv_unpack_kernel, gy, chips, place_of),
        [tv_half, tv_half],
        [scratch(2 * depth + 5, half, columns)],
        scalars,
        *tv_in,
    )
    tv_got = lax.ppermute(tv_give, AXES, near)

    wide = (depth + 6, rows, columns)
    out_half = (2, depth, half, columns)
    keep, give = call(
        functools.partial(flow_kernel, slabs * depth, place_of),
        [out_half, out_half],
        [scratch(depth + 6, 2, rows, columns), scratch(depth + 5, rows, columns)]
        + [scratch(*wide)] * 9
        + [scratch(2, depth, rows, columns)],
        scalars,
        own,
        near_in,
        far_in,
        tv_own,
        tv_got,
        mib=16,
    )
    got = lax.ppermute(give, AXES, near)
    messages = call(
        functools.partial(pack_kernel, gy, place_of),
        [(2, 2 * depth, block_rows, block_columns)] * chips,
        [],
        scalars,
        keep,
        got,
    )
    arrived = [lax.ppermute(piece, AXES, routes[k]) for k, piece in enumerate(messages)]
    labels, source_flow = call(
        functools.partial(unpack_kernel, chips, place_of),
        [tv_weight.shape, tv_weight.shape],
        [],
        scalars,
        *arrived,
    )
    return (labels, source_flow)


def shards(features, score_filter_weight, tv_weight):
    gx, gy, gz = (lax.axis_size(axis) for axis in AXES)
    chips = gy * gz // 2
    fits = (
        features.shape[1] == 4
        and gx == gz
        and gx % 2 == 0
        and chips & (chips - 1) == 0
        and tv_weight.shape[1] % 8 == 0
        and tv_weight.shape[2] % 128 == 0
    )
    return (on_slabs if fits else on_bricks)(features, score_filter_weight, tv_weight)


def solution(mesh):
    return jax.shard_map(
        shards,
        mesh=mesh,
        in_specs=(P(None, ("gx", "gy", "gz"), None, None), P(), P("gz", "gx", "gy")),
        out_specs=(P("gz", "gx", "gy"), P("gz", "gx", "gy")),
        check_vma=False,
    )
```

```python
import functools

import jax
import jax.numpy as jnp
from jax import lax
from jax.experimental import pallas as pl
from jax.experimental.pallas import tpu as pltpu
from jax.sharding import PartitionSpec as P

ITERS = 3
AXES = ("gx", "gy", "gz")

penalty = 0.3
step_size = 0.11
TV_MIDDLE, TV_SPREAD, TV_BINADES = 0.275, 0.225, 120.0
inverse_penalty = 1.0 / penalty


VMEM = pl.BlockSpec(memory_space=pltpu.VMEM)
SMEM = pl.BlockSpec(memory_space=pltpu.SMEM)


def with_halo(shard, sides, width):
    for axis, dim in sides:
        peers, length = (lax.axis_size(axis), shard.shape[dim])
        up = [(i, (i + 1) % peers) for i in range(peers - 1)]
        down = [(j, i) for i, j in up]
        last = lax.slice_in_dim(shard, length - width, length, axis=dim)
        leading = lax.slice_in_dim(shard, 0, width, axis=dim)
        before = lax.ppermute(last, axis, up)
        after = lax.ppermute(leading, axis, down)
        shard = jnp.concatenate([before, shard, after], axis=dim)
    return shard


def moved(values, offset, axis_id):
    if offset == 0:
        return values
    length = values.shape[axis_id]
    empty_border = jnp.zeros_like(lax.slice_in_dim(values, 0, 1, axis=axis_id))
    if offset > 0:
        return jnp.concatenate(
            [lax.slice_in_dim(values, 1, length, axis=axis_id), empty_border], axis_id
        )
    return jnp.concatenate(
        [empty_border, lax.slice_in_dim(values, 0, length - 1, axis=axis_id)], axis_id
    )


def plane_taps(slab, weights):
    kernel = jnp.transpose(weights, (2, 3, 0, 1)).reshape(18, weights.shape[1])
    products = jnp.einsum("kc,czxy->kzxy", kernel, slab, preferred_element_type=jnp.float32)
    products = products.reshape((3, 3, 2) + slab.shape[1:])
    summed = None
    for row_tap in range(3):
        for column_tap in range(3):
            term = moved(moved(products[row_tap, column_tap], row_tap - 1, 2), column_tap - 1, 3)
            summed = term if summed is None else summed + term
    return summed


def on_bricks(features, score_filter_weight, tv_weight):
    depth_len = features.shape[1]
    padded = with_halo(features, ((AXES, 1),), 1)
    response = None
    for depth_tap in range(3):
        window = lax.slice_in_dim(padded, depth_tap, depth_tap + depth_len, axis=1)
        term = plane_taps(window, score_filter_weight[:, :, depth_tap])
        response = term if response is None else response + term
    lifted = response.reshape((2, 1, 1) + response.shape[1:])
    by_plane = lax.all_to_all(
        lax.all_to_all(lifted, "gx", split_axis=4, concat_axis=1, tiled=True),
        "gy",
        split_axis=5,
        concat_axis=2,
        tiled=True,
    )
    edge_capacity = jax.nn.softplus(by_plane)
    sorted_by_depth = lax.all_to_all(edge_capacity, "gz", split_axis=1, concat_axis=3, tiled=True)
    brick = sorted_by_depth.reshape(
        (
            2,
            sorted_by_depth.shape[2] * sorted_by_depth.shape[3],
            sorted_by_depth.shape[4],
            sorted_by_depth.shape[5],
        )
    )
    source_cap = brick[0]
    sink_cap = brick[1]
    grid_shape = source_cap.shape
    starts = (
        lax.axis_index("gz") * grid_shape[0],
        lax.axis_index("gx") * grid_shape[1],
        lax.axis_index("gy") * grid_shape[2],
    )
    totals = (
        grid_shape[0] * lax.axis_size("gz"),
        grid_shape[1] * lax.axis_size("gx"),
        grid_shape[2] * lax.axis_size("gy"),
    )
    region = tuple((length + 1 for length in grid_shape))
    inside = []
    for axis_id in range(3):
        position = starts[axis_id] - 1 + lax.broadcasted_iota(jnp.int32, region, axis_id)
        inside.append((position >= 0) & (position <= totals[axis_id] - 2))
    source_flow = jnp.minimum(source_cap, sink_cap)
    sink_flow = source_flow
    labels = jax.nn.sigmoid(source_cap - sink_cap)
    divergence = jnp.zeros(grid_shape, jnp.float32)
    edge_flows = [jnp.zeros(grid_shape, jnp.float32) for axis_id in range(3)]
    for iteration in range(ITERS):
        pressure = divergence - (source_flow - sink_flow + labels / penalty)
        state = jnp.stack([pressure, edge_flows[0], edge_flows[1], edge_flows[2], tv_weight], 0)
        widened_block = with_halo(state, (("gx", 2), ("gy", 3), ("gz", 1)), 1)
        base = widened_block[:, :-1, :-1, :-1]
        updated = []
        for axis_id in range(3):
            picks = [slice(0, -1), slice(0, -1), slice(0, -1)]
            picks[axis_id] = slice(1, None)
            next_pressure = widened_block[0][tuple(picks)]
            shifted = base[1 + axis_id] + step_size * (next_pressure - base[0])
            updated.append(jnp.where(inside[axis_id], shifted, jnp.float32(0.0)))
        flow_magnitude = jnp.sqrt(
            updated[0] * updated[0] + updated[1] * updated[1] + updated[2] * updated[2]
        )
        factor = base[4] / jnp.maximum(flow_magnitude, base[4])
        projected = [
            jnp.where(inside[axis_id], updated[axis_id] * factor, jnp.float32(0.0))
            for axis_id in range(3)
        ]
        edge_flows = [flow_part[1:, 1:, 1:] for flow_part in projected]
        divergence = (
            edge_flows[0]
            - projected[0][:-1, 1:, 1:]
            + (edge_flows[1] - projected[1][1:, :-1, 1:])
            + (edge_flows[2] - projected[2][1:, 1:, :-1])
        )
        source_flow = jnp.minimum(
            divergence - labels / penalty + sink_flow + 1.0 / penalty, source_cap
        )
        sink_flow = jnp.minimum(-divergence + source_flow + labels / penalty, sink_cap)
        labels = labels - penalty * (divergence + sink_flow - source_flow)
    return (labels, source_flow)


def conv_kernel(place_of, index,  w_ref, f_ref, own_ref, near_ref, far_ref, band):
    channels, depth, rows, columns = f_ref.shape
    parity = lax.rem(place_of(index)[2], 2)
    width = channels * rows
    channel = lax.broadcasted_iota(jnp.int32, (channels, width), 0)
    position = lax.broadcasted_iota(jnp.int32, (channels, width), 1)
    spread = (position >= channel * rows) & (position < (channel + 1) * rows)
    spread = jnp.where(spread, 1.0, 0.0).astype(jnp.bfloat16)
    taps_of = w_ref[...].astype(jnp.float32).reshape(27 * 2, channels).astype(jnp.bfloat16)
    weights = jnp.dot(taps_of, spread, preferred_element_type=jnp.float32)
    column = lax.broadcasted_iota(jnp.int32, (rows, width), 1)
    offset = lax.rem(column, rows) - lax.broadcasted_iota(jnp.int32, (rows, width), 0)
    for dz in range(3):
        for j in range(3):
            for o in range(2):
                value = jnp.zeros((rows, width), jnp.float32)
                for i in range(3):
                    r = ((dz * 3 + i) * 3 + j) * 2 + o
                    value = jnp.where(offset == i - 1, weights[r : r + 1, :], value)
                start = (j * 2 + o) * rows
                band[dz, start : start + rows, :] = value.astype(jnp.bfloat16)
    lane = lax.broadcasted_iota(jnp.int32, (2 * rows, columns), 1)
    for z in range(-1, depth + 1):
        taps = None
        for dz in range(3):
            plane = z + dz - 1
            if 0 <= plane < depth:
                term = jnp.dot(
                    band[dz],
                    f_ref[:, plane].reshape(width, columns),
                    preferred_element_type=jnp.float32,
                )
                taps = term if taps is None else taps + term
        before = pltpu.roll(taps[: 2 * rows], 1, 1)
        after = pltpu.roll(taps[4 * rows :], columns - 1, 1)
        total = (
            taps[2 * rows : 4 * rows]
            + jnp.where(lane >= 1, before, 0.0)
            + jnp.where(lane < columns - 1, after, 0.0)
        )
        own_ref[z + 1] = total.reshape(2, rows, columns)
    near_ref[...] = own_ref[pl.ds(2 - 2 * parity, depth)]
    far_ref[...] = own_ref[pl.ds(2 * parity, depth)]


def softplus(v):
    e = jnp.exp(-jnp.abs(v))
    series = e * (1.0 - e * (0.5 - e * (1.0 / 3.0 - e * 0.25)))
    return jnp.maximum(v, 0.0) + jnp.where(e < 0.02, series, jnp.log(1.0 + e))


def flow_kernel(
    total_depth,
    place_of,
    block_rows,
    index,
    own_ref,
    near_ref,
    far_ref,
    tv_own_ref,
    tv_got_ref,
    keep_ref,
    give_ref,
    resp,
    tv,
    cap_s,
    cap_t,
    flow_s,
    flow_t,
    lab,
    press,
    q0,
    q1,
    q2,
    out,
):
    planes, _, rows, columns = own_ref.shape
    depth = planes - 2
    pairs = rows // (2 * block_rows)
    parity = lax.rem(place_of(index)[2], 2)
    first = index[0] * depth
    resp[3 - 1 : 3 + depth + 1] = own_ref[...]
    resp[0:2] = jnp.zeros((2, 2, rows, columns), jnp.float32)
    resp[depth + 4 : depth + 6] = jnp.zeros((2, 2, rows, columns), jnp.float32)
    near_at = depth + 2 - (depth + 2) * parity
    far_at = (depth + 2) * parity
    resp[pl.ds(near_at, 4)] = resp[pl.ds(near_at, 4)] + near_ref[...]
    resp[pl.ds(far_at, 4)] = resp[pl.ds(far_at, 4)] + far_ref[...]
    for t in range(pairs):
        at = pl.ds(t * block_rows, block_rows)
        tv[:, at_block(2 * t + 1 - parity, block_rows), :] = tv_own_ref[:, at, :]
        tv[:, at_block(2 * t + parity, block_rows), :] = tv_got_ref[:, at, :]

    def start(i, carry):
        source_cap = softplus(resp[i, 0])
        sink_cap = softplus(resp[i, 1])
        flow = jnp.minimum(source_cap, sink_cap)
        labels = jax.nn.sigmoid(source_cap - sink_cap)
        cap_s[i] = source_cap
        cap_t[i] = sink_cap
        flow_s[i] = flow
        flow_t[i] = flow
        lab[i] = labels
        press[i] = -(labels * inverse_penalty)
        return carry

    lax.fori_loop(0, depth + 6, start, 0)
    row = lax.broadcasted_iota(jnp.int32, (rows, columns), 0)
    column = lax.broadcasted_iota(jnp.int32, (rows, columns), 1)
    row_in = row < rows - 1
    column_in = column < columns - 1

    def edges(i, fresh):
        z = first + i - 3
        p = press[i]
        deep = step_size * (press[i + 1] - p)
        down = step_size * (pltpu.roll(p, rows - 1, 0) - p)
        right = step_size * (pltpu.roll(p, columns - 1, 1) - p)
        if not fresh:
            deep, down, right = q0[i] + deep, q1[i] + down, q2[i] + right
        inside = (z >= 0) & (z < total_depth - 1)
        deep = jnp.where(inside, deep, 0.0)
        down = jnp.where(row_in, down, 0.0)
        right = jnp.where(column_in, right, 0.0)
        weight = tv[i]
        squares = deep * deep + down * down + right * right
        factor = jnp.minimum(weight * lax.rsqrt(squares), 1.0)
        deep, down, right = deep * factor, down * factor, right * factor
        deep = jnp.where(inside, deep, 0.0)
        q0[i] = deep
        q1[i] = down
        q2[i] = right
        return deep, down, right

    def cell(i, fresh, last):
        deep, down, right = edges(i, fresh)
        divergence = (
            deep - q0[i - 1] + (down - pltpu.roll(down, 1, 0)) + (right - pltpu.roll(right, 1, 1))
        )
        labels = lab[i]
        scaled = labels * inverse_penalty
        source_flow = jnp.minimum(divergence - scaled + flow_t[i] + inverse_penalty, cap_s[i])
        sink_flow = jnp.minimum(-divergence + source_flow + scaled, cap_t[i])
        labels = labels - penalty * (divergence + sink_flow - source_flow)
        if last:
            out[0, i - 3] = labels
            out[1, i - 3] = source_flow
        else:
            flow_t[i] = sink_flow
            lab[i] = labels
            press[i] = divergence - (source_flow - sink_flow + labels * inverse_penalty)

    for iteration in range(ITERS):
        fresh, last = iteration == 0, iteration == ITERS - 1
        edges(iteration, fresh)

        def step(i, carry):
            cell(i, fresh, last)
            return carry

        lax.fori_loop(iteration + 1, depth + 5 - iteration, step, 0)
    for t in range(pairs):
        at = pl.ds(t * block_rows, block_rows)
        keep_ref[:, :, at, :] = out[:, :, at_block(2 * t + 1 - parity, block_rows), :]
        give_ref[:, :, at, :] = out[:, :, at_block(2 * t + parity, block_rows), :]


def pack_kernel(rounds, sizes, index, keep_ref, got_ref, *message_refs):
    depth = keep_ref.shape[1]
    _, _, block_rows, block_columns = message_refs[0].shape
    _, b, c = places(sizes, index)
    parity = lax.rem(c, 2)
    for (kz, ky), message in zip(rounds, message_refs):
        rows = at_block(lax.div(lax.rem(c + kz, sizes[2]), 2), block_rows)
        columns = at_block(lax.rem(b + ky, sizes[1]), block_columns)
        message[:, pl.ds(parity * depth, depth)] = keep_ref[:, :, rows, columns]
        message[:, pl.ds(depth - parity * depth, depth)] = got_ref[:, :, rows, columns]


def chip_of(sizes, index, kz, ky):
    a, b, _ = places(sizes, index)
    _, gy, gz = sizes
    return lax.rem(b + gy - ky, gy) * (gz // 2) + lax.div(lax.rem(a + gz - kz, gz), 2)


def unpack_kernel(rounds, sizes, index, *refs):
    messages, (labels_ref, flow_ref) = refs[: len(rounds)], refs[len(rounds) :]
    planes = messages[0].shape[1]
    for (kz, ky), message in zip(rounds, messages):
        at = pl.ds(chip_of(sizes, index, kz, ky) * planes, planes)
        labels_ref[at] = message[0]
        flow_ref[at] = message[1]


def encode(values):
    scaled = (values - TV_MIDDLE) * (1.0 / TV_SPREAD)
    steps = jnp.abs(scaled) * TV_BINADES
    binade = jnp.floor(steps)
    size = jnp.exp2(binade - TV_BINADES / 2) * (1.0 + (steps - binade))
    return jnp.where(scaled < 0.0, -size, size).astype(jnp.bfloat16)


def decode(codes):
    codes = codes.astype(jnp.float32)
    size = jnp.abs(codes)
    binade = jnp.floor(jnp.log2(size))
    steps = binade + (size * jnp.exp2(-binade) - 1.0) + TV_BINADES / 2
    scaled = steps * (TV_SPREAD / TV_BINADES)
    return TV_MIDDLE + jnp.where(codes < 0.0, -scaled, scaled)


def tv_pack_kernel(rounds, sizes, index, tv_ref, near_ref, far_ref, *refs):
    messages, wide = refs[:-1], refs[-1]
    length = tv_ref.shape[0]
    parity = lax.rem(places(sizes, index)[2], 2)
    wide[3 : 3 + length] = tv_ref[...]

    @pl.when(parity == 0)
    def _():
        wide[length + 3 : length + 6] = near_ref[...]
        wide[0:3] = far_ref[...]

    @pl.when(parity == 1)
    def _():
        wide[length + 3 : length + 6] = far_ref[...]
        wide[0:3] = near_ref[...]

    planes = messages[0].shape[0]
    for (kz, ky), message in zip(rounds, messages):
        at = pl.ds(chip_of(sizes, index, kz, ky) * (planes - 5), planes)
        message[...] = encode(wide[at])


def tv_unpack_kernel(rounds, sizes, index, *refs):
    messages, (own_ref, give_ref, full) = refs[: len(rounds)], refs[len(rounds) :]
    planes, block_rows, block_columns = messages[0].shape
    depth = (planes - 5) // 2
    _, b, c = places(sizes, index)
    parity = lax.rem(c, 2)
    for (kz, ky), message in zip(rounds, messages):
        rows = at_block(lax.div(lax.rem(c + kz, sizes[2]), 2), block_rows)
        columns = at_block(lax.rem(b + ky, sizes[1]), block_columns)
        full[:, rows, columns] = decode(message[...])
    own_ref[...] = full[pl.ds(parity * depth, depth + 5)]
    give_ref[...] = full[pl.ds(depth - parity * depth, depth + 5)]


def places(sizes, index_ref):
    gx, gy, gz = sizes
    slab = index_ref[0]
    return (
        lax.div(slab, gy * gz),
        lax.rem(lax.div(slab, gz), gy),
        lax.rem(slab, gz),
    )


def at_block(block, length):
    return pl.ds(pl.multiple_of(block * length, length), length)


def call(kernel, out_shape, scratch, scalars, *operands, mib=8, dtype=jnp.float32):
    return pl.pallas_call(
        kernel,
        out_shape=[jax.ShapeDtypeStruct(shape, dtype) for shape in out_shape],
        in_specs=[SMEM] + [VMEM] * len(operands),
        out_specs=[VMEM] * len(out_shape),
        scratch_shapes=scratch,
        compiler_params=pltpu.CompilerParams(vmem_limit_bytes=mib * 1024 * 1024),
    )(scalars, *operands)


def scratch(*shape, dtype=jnp.float32):
    return pltpu.VMEM(shape, dtype)


def on_slabs(features, score_filter_weight, tv_weight):
    channels, depth, rows, columns = features.shape
    brick_depth, block_rows, block_columns = tv_weight.shape
    gx, gy, gz = (lax.axis_size(axis) for axis in AXES)
    slabs = gx * gy * gz
    half = rows // 2
    c = lax.axis_index("gz")
    sizes = (gx, gy, gz)
    place_of = functools.partial(places, sizes)
    scalars = lax.axis_index(AXES).astype(jnp.int32).reshape(1)

    near = [(s, s ^ 1) for s in range(slabs)]
    far = [(s, s + 1) for s in range(1, slabs - 1, 2)]
    far = far + [(t, s) for s, t in far]
    gz_near = [(s, s ^ 1) for s in range(gz)]
    gz_far = [(s, s + 1) for s in range(1, gz - 1, 2)]
    gz_far = gz_far + [(t, s) for s, t in gz_far]

    def place(i, j, k):
        return (i * gy + j) * gz + k

    def to_bricks(kz, ky):
        return [
            (place(i, j, k), place((k + kz) % gz, (j + ky) % gy, i))
            for i in range(gx)
            for j in range(gy)
            for k in range(gz)
        ]

    odd = range(1, gz, 2)
    rounds = [(kz, ky) for kz in odd for ky in range(gy)]
    tv_rounds = [(kz, ky) for ky in reversed(range(gy)) for kz in odd]

    tv_last, tv_first = tv_weight[brick_depth - 3 :], tv_weight[:3]
    even = c % 2 == 0
    tv_near = lax.ppermute(jnp.where(even, tv_last, tv_first), "gz", gz_near)
    tv_far = lax.ppermute(jnp.where(even, tv_first, tv_last), "gz", gz_far)
    tv_messages = call(
        functools.partial(tv_pack_kernel, tv_rounds, sizes),
        [(2 * depth + 5, block_rows, block_columns)] * len(tv_rounds),
        [scratch(brick_depth + 6, block_rows, block_columns)],
        scalars,
        tv_weight,
        tv_near,
        tv_far,
        dtype=jnp.bfloat16,
    )

    flat_weight = jnp.transpose(score_filter_weight, (2, 3, 4, 0, 1))
    message = (4, 2, rows, columns)
    own, near_out, far_out = call(
        functools.partial(conv_kernel, place_of),
        [(depth + 2, 2, rows, columns), message, message],
        [scratch(3, 6 * rows, channels * rows, dtype=jnp.bfloat16)],
        scalars,
        flat_weight,
        features,
        mib=14,
    )
    tv_messages, far_out, near_out = lax.optimization_barrier((tv_messages, far_out, near_out))
    far_in = lax.ppermute(far_out, AXES, far)
    near_in = lax.ppermute(near_out, AXES, near)

    tv_in = [
        lax.ppermute(piece, AXES, [(t, s) for s, t in to_bricks(*shift)])
        for shift, piece in zip(tv_rounds, tv_messages)
    ]
    tv_half = (depth + 5, half, columns)
    tv_own, tv_give = call(
        functools.partial(tv_unpack_kernel, tv_rounds, sizes),
        [tv_half, tv_half],
        [scratch(2 * depth + 5, half, columns)],
        scalars,
        *tv_in,
    )
    tv_got = lax.ppermute(tv_give, AXES, near)

    wide = (depth + 6, rows, columns)
    out_half = (2, depth, half, columns)
    keep, give = call(
        functools.partial(flow_kernel, slabs * depth, place_of, block_rows),
        [out_half, out_half],
        [scratch(depth + 6, 2, rows, columns), scratch(depth + 5, rows, columns)]
        + [scratch(*wide)] * 9
        + [scratch(2, depth, rows, columns)],
        scalars,
        own,
        near_in,
        far_in,
        tv_own,
        tv_got,
        mib=16,
    )
    got = lax.ppermute(give, AXES, near)
    messages = call(
        functools.partial(pack_kernel, rounds, sizes),
        [(2, 2 * depth, block_rows, block_columns)] * len(rounds),
        [],
        scalars,
        keep,
        got,
    )
    arrived = [
        lax.ppermute(piece, AXES, to_bricks(*shift)) for shift, piece in zip(rounds, messages)
    ]
    labels, source_flow = call(
        functools.partial(unpack_kernel, rounds, sizes),
        [tv_weight.shape, tv_weight.shape],
        [],
        scalars,
        *arrived,
    )
    return (labels, source_flow)


def shards(features, score_filter_weight, tv_weight):
    gx, gy, gz = (lax.axis_size(axis) for axis in AXES)
    fits = (
        features.shape[1] == 4
        and gx == gz
        and gx % 2 == 0
        and tv_weight.shape[1] % 8 == 0
        and tv_weight.shape[2] % 128 == 0
    )
    return (on_slabs if fits else on_bricks)(features, score_filter_weight, tv_weight)


def solution(mesh):
    return jax.shard_map(
        shards,
        mesh=mesh,
        in_specs=(P(None, ("gx", "gy", "gz"), None, None), P(), P("gz", "gx", "gy")),
        out_specs=(P("gz", "gx", "gy"), P("gz", "gx", "gy")),
        check_vma=False,
    )
```

```python
import functools

import jax
import jax.numpy as jnp
from jax import lax
from jax.experimental import pallas as pl
from jax.experimental.pallas import tpu as pltpu
from jax.sharding import PartitionSpec as P

ITERS = 3
AXES = ("gx", "gy", "gz")

penalty = 0.3
step_size = 0.11
TV_MIDDLE, TV_SPREAD, TV_BINADES = 0.275, 0.225, 120.0
RANGE, BINADES = 7.0, 240.0
inverse_penalty = 1.0 / penalty


VMEM = pl.BlockSpec(memory_space=pltpu.VMEM)
SMEM = pl.BlockSpec(memory_space=pltpu.SMEM)


def with_halo(shard, sides, width):
    for axis, dim in sides:
        peers, length = (lax.axis_size(axis), shard.shape[dim])
        up = [(i, (i + 1) % peers) for i in range(peers - 1)]
        down = [(j, i) for i, j in up]
        last = lax.slice_in_dim(shard, length - width, length, axis=dim)
        leading = lax.slice_in_dim(shard, 0, width, axis=dim)
        before = lax.ppermute(last, axis, up)
        after = lax.ppermute(leading, axis, down)
        shard = jnp.concatenate([before, shard, after], axis=dim)
    return shard


def moved(values, offset, axis_id):
    if offset == 0:
        return values
    length = values.shape[axis_id]
    empty_border = jnp.zeros_like(lax.slice_in_dim(values, 0, 1, axis=axis_id))
    if offset > 0:
        return jnp.concatenate(
            [lax.slice_in_dim(values, 1, length, axis=axis_id), empty_border], axis_id
        )
    return jnp.concatenate(
        [empty_border, lax.slice_in_dim(values, 0, length - 1, axis=axis_id)], axis_id
    )


def plane_taps(slab, weights):
    kernel = jnp.transpose(weights, (2, 3, 0, 1)).reshape(18, weights.shape[1])
    products = jnp.einsum("kc,czxy->kzxy", kernel, slab, preferred_element_type=jnp.float32)
    products = products.reshape((3, 3, 2) + slab.shape[1:])
    summed = None
    for row_tap in range(3):
        for column_tap in range(3):
            term = moved(moved(products[row_tap, column_tap], row_tap - 1, 2), column_tap - 1, 3)
            summed = term if summed is None else summed + term
    return summed


def on_bricks(features, score_filter_weight, tv_weight):
    depth_len = features.shape[1]
    padded = with_halo(features, ((AXES, 1),), 1)
    response = None
    for depth_tap in range(3):
        window = lax.slice_in_dim(padded, depth_tap, depth_tap + depth_len, axis=1)
        term = plane_taps(window, score_filter_weight[:, :, depth_tap])
        response = term if response is None else response + term
    lifted = response.reshape((2, 1, 1) + response.shape[1:])
    by_plane = lax.all_to_all(
        lax.all_to_all(lifted, "gx", split_axis=4, concat_axis=1, tiled=True),
        "gy",
        split_axis=5,
        concat_axis=2,
        tiled=True,
    )
    edge_capacity = jax.nn.softplus(by_plane)
    sorted_by_depth = lax.all_to_all(edge_capacity, "gz", split_axis=1, concat_axis=3, tiled=True)
    brick = sorted_by_depth.reshape(
        (
            2,
            sorted_by_depth.shape[2] * sorted_by_depth.shape[3],
            sorted_by_depth.shape[4],
            sorted_by_depth.shape[5],
        )
    )
    source_cap = brick[0]
    sink_cap = brick[1]
    grid_shape = source_cap.shape
    starts = (
        lax.axis_index("gz") * grid_shape[0],
        lax.axis_index("gx") * grid_shape[1],
        lax.axis_index("gy") * grid_shape[2],
    )
    totals = (
        grid_shape[0] * lax.axis_size("gz"),
        grid_shape[1] * lax.axis_size("gx"),
        grid_shape[2] * lax.axis_size("gy"),
    )
    region = tuple((length + 1 for length in grid_shape))
    inside = []
    for axis_id in range(3):
        position = starts[axis_id] - 1 + lax.broadcasted_iota(jnp.int32, region, axis_id)
        inside.append((position >= 0) & (position <= totals[axis_id] - 2))
    source_flow = jnp.minimum(source_cap, sink_cap)
    sink_flow = source_flow
    labels = jax.nn.sigmoid(source_cap - sink_cap)
    divergence = jnp.zeros(grid_shape, jnp.float32)
    edge_flows = [jnp.zeros(grid_shape, jnp.float32) for axis_id in range(3)]
    for iteration in range(ITERS):
        pressure = divergence - (source_flow - sink_flow + labels / penalty)
        state = jnp.stack([pressure, edge_flows[0], edge_flows[1], edge_flows[2], tv_weight], 0)
        widened_block = with_halo(state, (("gx", 2), ("gy", 3), ("gz", 1)), 1)
        base = widened_block[:, :-1, :-1, :-1]
        updated = []
        for axis_id in range(3):
            picks = [slice(0, -1), slice(0, -1), slice(0, -1)]
            picks[axis_id] = slice(1, None)
            next_pressure = widened_block[0][tuple(picks)]
            shifted = base[1 + axis_id] + step_size * (next_pressure - base[0])
            updated.append(jnp.where(inside[axis_id], shifted, jnp.float32(0.0)))
        flow_magnitude = jnp.sqrt(
            updated[0] * updated[0] + updated[1] * updated[1] + updated[2] * updated[2]
        )
        factor = base[4] / jnp.maximum(flow_magnitude, base[4])
        projected = [
            jnp.where(inside[axis_id], updated[axis_id] * factor, jnp.float32(0.0))
            for axis_id in range(3)
        ]
        edge_flows = [flow_part[1:, 1:, 1:] for flow_part in projected]
        divergence = (
            edge_flows[0]
            - projected[0][:-1, 1:, 1:]
            + (edge_flows[1] - projected[1][1:, :-1, 1:])
            + (edge_flows[2] - projected[2][1:, 1:, :-1])
        )
        source_flow = jnp.minimum(
            divergence - labels / penalty + sink_flow + 1.0 / penalty, source_cap
        )
        sink_flow = jnp.minimum(-divergence + source_flow + labels / penalty, sink_cap)
        labels = labels - penalty * (divergence + sink_flow - source_flow)
    return (labels, source_flow)


def band_kernel(rows, index, w_ref, band):
    channels = w_ref.shape[-1]
    width = channels * rows
    channel = lax.broadcasted_iota(jnp.int32, (channels, width), 0)
    position = lax.broadcasted_iota(jnp.int32, (channels, width), 1)
    spread = (position >= channel * rows) & (position < (channel + 1) * rows)
    spread = jnp.where(spread, 1.0, 0.0).astype(jnp.bfloat16)
    taps_of = w_ref[...].astype(jnp.float32).reshape(27 * 2, channels).astype(jnp.bfloat16)
    weights = jnp.dot(taps_of, spread, preferred_element_type=jnp.float32)
    column = lax.broadcasted_iota(jnp.int32, (rows, width), 1)
    offset = lax.rem(column, rows) - lax.broadcasted_iota(jnp.int32, (rows, width), 0)
    for dz in range(3):
        for j in range(3):
            for o in range(2):
                value = jnp.zeros((rows, width), jnp.float32)
                for i in range(3):
                    r = ((dz * 3 + i) * 3 + j) * 2 + o
                    value = jnp.where(offset == i - 1, weights[r : r + 1, :], value)
                start = (j * 2 + o) * rows
                band[dz, start : start + rows, :] = value.astype(jnp.bfloat16)


def conv_kernel(place_of, index, band, f_ref, own_ref, near_ref, far_ref):
    channels, depth, rows, columns = f_ref.shape
    parity = lax.rem(place_of(index)[2], 2)
    width = channels * rows
    lane = lax.broadcasted_iota(jnp.int32, (2 * rows, columns), 1)
    for z in range(-1, depth + 1):
        taps = None
        for dz in range(3):
            plane = z + dz - 1
            if 0 <= plane < depth:
                term = jnp.dot(
                    band[dz],
                    f_ref[:, plane].reshape(width, columns),
                    preferred_element_type=jnp.float32,
                )
                taps = term if taps is None else taps + term
        before = pltpu.roll(taps[: 2 * rows], 1, 1)
        after = pltpu.roll(taps[4 * rows :], columns - 1, 1)
        total = (
            taps[2 * rows : 4 * rows]
            + jnp.where(lane >= 1, before, 0.0)
            + jnp.where(lane < columns - 1, after, 0.0)
        )
        own_ref[z + 1] = total.reshape(2, rows, columns)
    for k in range(2):
        apart = softplus(own_ref[k + 2, 0]) - softplus(own_ref[k + 2, 1])
        near_ref[k] = apart
        far_ref[k] = apart
    near = depth - depth * parity
    far = depth * parity
    for k in range(2):
        near_ref[2 + 2 * k : 4 + 2 * k] = own_ref[near + k]
        far_ref[2 + 2 * k : 4 + 2 * k] = own_ref[far + k]


def to_code(steps, negative, binades):
    binade = jnp.floor(steps)
    size = jnp.exp2(binade - binades / 2) * (1.0 + (steps - binade))
    return jnp.where(negative, -size, size).astype(jnp.bfloat16)


def from_code(codes, binades):
    codes = codes.astype(jnp.float32)
    size = jnp.abs(codes)
    binade = jnp.floor(jnp.log2(size))
    return binade + (size * jnp.exp2(-binade) - 1.0) + binades / 2, codes < 0.0


def encode_tv(values):
    scaled = (values - TV_MIDDLE) * (1.0 / TV_SPREAD)
    return to_code(jnp.abs(scaled) * TV_BINADES, scaled < 0.0, TV_BINADES)


def decode_tv(codes):
    steps, negative = from_code(codes, TV_BINADES)
    scaled = steps * (TV_SPREAD / TV_BINADES)
    return TV_MIDDLE + jnp.where(negative, -scaled, scaled)


def encode(values, inverse_scale):
    size = jnp.abs(values) * inverse_scale
    binade = jnp.maximum(jnp.floor(jnp.log2(size)), -RANGE)
    steps = binade + RANGE + size * jnp.exp2(-binade)
    return to_code(steps * (BINADES / (RANGE + 1)), values < 0.0, BINADES)


def decode(codes, scale):
    steps, negative = from_code(codes, BINADES)
    steps = steps * ((RANGE + 1) / BINADES)
    binade = jnp.maximum(jnp.floor(steps) - 1.0, 0.0)
    size = (steps - binade) * jnp.exp2(binade - RANGE) * scale
    return jnp.where(negative, -size, size)


def softplus(v):
    e = jnp.exp(-jnp.abs(v))
    series = e * (1.0 - e * (0.5 - e * (1.0 / 3.0 - e * 0.25)))
    return jnp.maximum(v, 0.0) + jnp.where(e < 0.02, series, jnp.log(1.0 + e))


def flow_kernel(
    total_depth,
    place_of,
    block_rows,
    index,
    own_ref,
    near_ref,
    far_ref,
    tv_own_ref,
    tv_got_ref,
    keep_ref,
    give_ref,
    tv,
    cap_s,
    cap_t,
    flow_s,
    flow_t,
    lab,
    press,
    q0,
    q1,
    q2,
    out,
    codes,
):
    planes, _, rows, columns = own_ref.shape
    depth = planes - 2
    pairs = rows // (2 * block_rows)
    parity = lax.rem(place_of(index)[2], 2)
    first = index[0] * depth
    for t in range(pairs):
        at = pl.ds(t * block_rows, block_rows)
        tv[:, at_block(2 * t + 1 - parity, block_rows), :] = tv_own_ref[:, at, :]
        tv[:, at_block(2 * t + parity, block_rows), :] = tv_got_ref[:, at, :]

    def begin(i, source_cap, sink_cap, labels):
        flow = jnp.minimum(source_cap, sink_cap)
        cap_s[i] = source_cap
        cap_t[i] = sink_cap
        flow_s[i] = flow
        flow_t[i] = flow
        lab[i] = labels
        press[i] = -(labels * inverse_penalty)

    def begin_at(i, response):
        source_cap = softplus(response[0])
        sink_cap = softplus(response[1])
        begin(i, source_cap, sink_cap, jax.nn.sigmoid(source_cap - sink_cap))

    for z in range(1, depth - 1):
        begin_at(z + 3, own_ref[z + 1])

    def beyond(came, base, edge):
        for k in range(2):
            apart = came[k]
            zero = jnp.zeros_like(apart)
            begin(
                edge + k,
                jnp.maximum(apart, zero),
                jnp.maximum(-apart, zero),
                jax.nn.sigmoid(apart),
            )
            begin_at(base + k + 2, own_ref[base + k] + came[2 + 2 * k : 4 + 2 * k])

    above = depth + 4
    beyond(near_ref, depth - depth * parity, above - above * parity)
    beyond(far_ref, depth * parity, above * parity)
    row = lax.broadcasted_iota(jnp.int32, (rows, columns), 0)
    column = lax.broadcasted_iota(jnp.int32, (rows, columns), 1)
    row_in = row < rows - 1
    column_in = column < columns - 1

    def edges(i, fresh):
        z = first + i - 3
        p = press[i]
        deep = step_size * (press[i + 1] - p)
        down = step_size * (pltpu.roll(p, rows - 1, 0) - p)
        right = step_size * (pltpu.roll(p, columns - 1, 1) - p)
        if not fresh:
            deep, down, right = q0[i] + deep, q1[i] + down, q2[i] + right
        inside = (z >= 0) & (z < total_depth - 1)
        deep = jnp.where(inside, deep, 0.0)
        down = jnp.where(row_in, down, 0.0)
        right = jnp.where(column_in, right, 0.0)
        weight = tv[i]
        squares = deep * deep + down * down + right * right
        factor = jnp.minimum(weight * lax.rsqrt(squares), 1.0)
        deep, down, right = deep * factor, down * factor, right * factor
        deep = jnp.where(inside, deep, 0.0)
        q0[i] = deep
        q1[i] = down
        q2[i] = right
        return deep, down, right

    def cell(i, fresh, last):
        deep, down, right = edges(i, fresh)
        divergence = (
            deep - q0[i - 1] + (down - pltpu.roll(down, 1, 0)) + (right - pltpu.roll(right, 1, 1))
        )
        labels = lab[i]
        scaled = labels * inverse_penalty
        source_flow = jnp.minimum(divergence - scaled + flow_t[i] + inverse_penalty, cap_s[i])
        sink_flow = jnp.minimum(-divergence + source_flow + scaled, cap_t[i])
        labels = labels - penalty * (divergence + sink_flow - source_flow)
        if last:
            out[0, i - 3] = labels
            out[1, i - 3] = source_flow
        else:
            flow_t[i] = sink_flow
            lab[i] = labels
            press[i] = divergence - (source_flow - sink_flow + labels * inverse_penalty)

    for iteration in range(ITERS):
        fresh, last = iteration == 0, iteration == ITERS - 1
        edges(iteration, fresh)

        def step(i, carry):
            cell(i, fresh, last)
            return carry

        lax.fori_loop(iteration + 1, depth + 5 - iteration, step, 0)
    scales = []
    for o in range(2):
        largest = jnp.max(jnp.max(jnp.abs(out[o]), axis=0), axis=(0, 1), keepdims=True)
        binade = jnp.floor(jnp.log2(jnp.maximum(largest, 1e-30))) + 1.0
        scales.append(jnp.exp2(binade))
        inverse = jnp.exp2(-binade)
        for z in range(depth):
            codes[o * depth + z] = encode(out[o, z], inverse)
    of_labels = lax.rem(lax.broadcasted_iota(jnp.int32, (rows, columns), 0), 8) < 4
    codes[2 * depth] = jnp.where(of_labels, scales[0], scales[1]).astype(jnp.bfloat16)
    for t in range(pairs):
        at = pl.ds(t * block_rows, block_rows)
        keep_ref[:, at, :] = codes[:, at_block(2 * t + 1 - parity, block_rows), :]
        give_ref[:, at, :] = codes[:, at_block(2 * t + parity, block_rows), :]


def pack_kernel(rounds, sizes, index, keep_ref, got_ref, *message_refs):
    depth = keep_ref.shape[0] // 2
    _, block_rows, block_columns = message_refs[0].shape
    _, b, c = places(sizes, index)
    parity = lax.rem(c, 2)
    low = lax.broadcasted_iota(jnp.int32, (block_rows, block_columns), 0) < 8
    mine = low == (parity == 0)
    for (kz, ky), message in zip(rounds, message_refs):
        rows = at_block(lax.div(lax.rem(c + kz, sizes[2]), 2), block_rows)
        columns = at_block(lax.rem(b + ky, sizes[1]), block_columns)
        for o in range(2):
            at = pl.ds(o * depth, depth)
            message[pl.ds((2 * o + parity) * depth, depth)] = keep_ref[at, rows, columns]
            message[pl.ds((2 * o + 1 - parity) * depth, depth)] = got_ref[at, rows, columns]
        ours = keep_ref[2 * depth, rows, columns].astype(jnp.float32)
        theirs = got_ref[2 * depth, rows, columns].astype(jnp.float32)
        message[4 * depth] = jnp.where(mine, ours, theirs).astype(jnp.bfloat16)


def chip_of(sizes, index, kz, ky):
    a, b, _ = places(sizes, index)
    _, gy, gz = sizes
    return lax.rem(b + gy - ky, gy) * (gz // 2) + lax.div(lax.rem(a + gz - kz, gz), 2)


def unpack_kernel(rounds, sizes, index, *refs):
    messages, outs = refs[: len(rounds)], refs[len(rounds) :]
    depth = messages[0].shape[0] // 4
    for (kz, ky), message in zip(rounds, messages):
        first = chip_of(sizes, index, kz, ky) * 2 * depth
        scales = message[4 * depth].astype(jnp.float32)
        for o, out_ref in enumerate(outs):
            for half in range(2):
                row = 8 * half + 4 * o
                scale = scales[row : row + 1, :]
                for z in range(depth):
                    at = half * depth + z
                    out_ref[first + at] = decode(message[2 * depth * o + at], scale)


def tv_pack_kernel(rounds, sizes, index, tv_ref, near_ref, far_ref, *refs):
    messages, wide = refs[:-1], refs[-1]
    length = tv_ref.shape[0]
    parity = lax.rem(places(sizes, index)[2], 2)
    wide[3 : 3 + length] = tv_ref[...]

    @pl.when(parity == 0)
    def _():
        wide[length + 3 : length + 6] = near_ref[...]
        wide[0:3] = far_ref[...]

    @pl.when(parity == 1)
    def _():
        wide[length + 3 : length + 6] = far_ref[...]
        wide[0:3] = near_ref[...]

    planes = messages[0].shape[0]
    for (kz, ky), message in zip(rounds, messages):
        at = pl.ds(chip_of(sizes, index, kz, ky) * (planes - 5), planes)
        message[...] = encode_tv(wide[at])


def tv_unpack_kernel(rounds, sizes, index, *refs):
    messages, (own_ref, give_ref, full) = refs[: len(rounds)], refs[len(rounds) :]
    planes, block_rows, block_columns = messages[0].shape
    depth = (planes - 5) // 2
    _, b, c = places(sizes, index)
    parity = lax.rem(c, 2)
    for (kz, ky), message in zip(rounds, messages):
        rows = at_block(lax.div(lax.rem(c + kz, sizes[2]), 2), block_rows)
        columns = at_block(lax.rem(b + ky, sizes[1]), block_columns)
        full[:, rows, columns] = decode_tv(message[...])
    own_ref[...] = full[pl.ds(parity * depth, depth + 5)]
    give_ref[...] = full[pl.ds(depth - parity * depth, depth + 5)]


def places(sizes, index_ref):
    gx, gy, gz = sizes
    slab = index_ref[0]
    return (
        lax.div(slab, gy * gz),
        lax.rem(lax.div(slab, gz), gy),
        lax.rem(slab, gz),
    )


def at_block(block, length):
    return pl.ds(pl.multiple_of(block * length, length), length)


def call(kernel, out_shape, scratch, scalars, *operands, mib=8, dtype=jnp.float32, cost=(1e6, 1e6)):
    return pl.pallas_call(
        kernel,
        out_shape=[jax.ShapeDtypeStruct(shape, dtype) for shape in out_shape],
        in_specs=[SMEM] + [VMEM] * len(operands),
        out_specs=[VMEM] * len(out_shape),
        scratch_shapes=scratch,
        cost_estimate=pl.CostEstimate(
            flops=int(cost[0]), bytes_accessed=int(cost[1]), transcendentals=0
        ),
        compiler_params=pltpu.CompilerParams(vmem_limit_bytes=mib * 1024 * 1024),
    )(scalars, *operands)


def scratch(*shape, dtype=jnp.float32):
    return pltpu.VMEM(shape, dtype)


def on_slabs(features, score_filter_weight, tv_weight):
    channels, depth, rows, columns = features.shape
    brick_depth, block_rows, block_columns = tv_weight.shape
    gx, gy, gz = (lax.axis_size(axis) for axis in AXES)
    slabs = gx * gy * gz
    half = rows // 2
    c = lax.axis_index("gz")
    sizes = (gx, gy, gz)
    place_of = functools.partial(places, sizes)
    scalars = lax.axis_index(AXES).astype(jnp.int32).reshape(1)

    near = [(s, s ^ 1) for s in range(slabs)]
    far = [(s, s + 1) for s in range(1, slabs - 1, 2)]
    far = far + [(t, s) for s, t in far]
    gz_near = [(s, s ^ 1) for s in range(gz)]
    gz_far = [(s, s + 1) for s in range(1, gz - 1, 2)]
    gz_far = gz_far + [(t, s) for s, t in gz_far]

    def place(i, j, k):
        return (i * gy + j) * gz + k

    def to_bricks(kz, ky):
        return [
            (place(i, j, k), place((k + kz) % gz, (j + ky) % gy, i))
            for i in range(gx)
            for j in range(gy)
            for k in range(gz)
        ]

    odd = range(1, gz, 2)
    rounds = [(kz, ky) for kz in odd for ky in range(gy)]
    tv_rounds = [(kz, ky) for ky in reversed(range(gy)) for kz in odd]

    tv_last, tv_first = tv_weight[brick_depth - 3 :], tv_weight[:3]
    even = c % 2 == 0
    tv_near = lax.ppermute(jnp.where(even, tv_last, tv_first), "gz", gz_near)
    tv_far = lax.ppermute(jnp.where(even, tv_first, tv_last), "gz", gz_far)
    tv_messages = call(
        functools.partial(tv_pack_kernel, tv_rounds, sizes),
        [(2 * depth + 5, block_rows, block_columns)] * len(tv_rounds),
        [scratch(brick_depth + 6, block_rows, block_columns)],
        scalars,
        tv_weight,
        tv_near,
        tv_far,
        dtype=jnp.bfloat16,
    )

    flat_weight = jnp.transpose(score_filter_weight, (2, 3, 4, 0, 1))
    (band,) = call(
        functools.partial(band_kernel, rows),
        [(3, 6 * rows, channels * rows)],
        [],
        scalars,
        flat_weight,
        dtype=jnp.bfloat16,
        cost=(1e9, 8e6),
    )
    message = (6, rows, columns)
    own, near_out, far_out = call(
        functools.partial(conv_kernel, place_of),
        [(depth + 2, 2, rows, columns), message, message],
        [],
        scalars,
        band,
        features,
        cost=(2.4e9, 4e6),
    )
    tv_messages, far_out, near_out = lax.optimization_barrier((tv_messages, far_out, near_out))
    far_in = lax.ppermute(far_out, AXES, far)
    near_in = lax.ppermute(near_out, AXES, near)

    tv_in = [
        lax.ppermute(piece, AXES, [(t, s) for s, t in to_bricks(*shift)])
        for shift, piece in zip(tv_rounds, tv_messages)
    ]
    tv_half = (depth + 5, half, columns)
    tv_own, tv_give = call(
        functools.partial(tv_unpack_kernel, tv_rounds, sizes),
        [tv_half, tv_half],
        [scratch(2 * depth + 5, half, columns)],
        scalars,
        *tv_in,
    )
    tv_got = lax.ppermute(tv_give, AXES, near)

    wide = (depth + 6, rows, columns)
    out_half = (2 * depth + 1, half, columns)
    keep, give = call(
        functools.partial(flow_kernel, slabs * depth, place_of, block_rows),
        [out_half, out_half],
        [scratch(depth + 5, rows, columns)]
        + [scratch(*wide)] * 9
        + [scratch(2, depth, rows, columns)]
        + [scratch(2 * depth + 1, rows, columns, dtype=jnp.bfloat16)],
        scalars,
        own,
        near_in,
        far_in,
        tv_own,
        tv_got,
        mib=16,
        dtype=jnp.bfloat16,
    )
    got = lax.ppermute(give, AXES, near)
    messages = call(
        functools.partial(pack_kernel, rounds, sizes),
        [(4 * depth + 1, block_rows, block_columns)] * len(rounds),
        [],
        scalars,
        keep,
        got,
        dtype=jnp.bfloat16,
    )
    arrived = [
        lax.ppermute(piece, AXES, to_bricks(*shift)) for shift, piece in zip(rounds, messages)
    ]
    labels, source_flow = call(
        functools.partial(unpack_kernel, rounds, sizes),
        [tv_weight.shape, tv_weight.shape],
        [],
        scalars,
        *arrived,
    )
    return (labels, source_flow)


def shards(features, score_filter_weight, tv_weight):
    gx, gy, gz = (lax.axis_size(axis) for axis in AXES)
    fits = (
        features.shape[1] == 4
        and gx == gz
        and gx % 2 == 0
        and tv_weight.shape[1] % 16 == 0
        and tv_weight.shape[2] % 128 == 0
    )
    return (on_slabs if fits else on_bricks)(features, score_filter_weight, tv_weight)


def solution(mesh):
    return jax.shard_map(
        shards,
        mesh=mesh,
        in_specs=(P(None, ("gx", "gy", "gz"), None, None), P(), P("gz", "gx", "gy")),
        out_specs=(P("gz", "gx", "gy"), P("gz", "gx", "gy")),
        check_vma=False,
    )
```
